128 devices in a mesh: ctx: 8 (over y, core), fsdp: 16 (over x, z).
Axes of the slice: x: 4, y: 4, z: 4, core: 2. Of those that a mesh axis runs over, the one named last changes fastest.
Arguments:
- hidden: bfloat16 [8, 16, 256, 2048], P('ctx', 'fsdp'), may hold values from -4.5 to 4.5
- norm_gain: float32 [2048], replicated, may hold values from 0.1 to 1.9
- w_query: bfloat16 [2048, 2048], P('fsdp', 'ctx'), may hold values from -1 to 1
- w_key: bfloat16 [2048, 1024], P('fsdp', 'ctx'), may hold values from -1 to 1
- w_value: bfloat16 [2048, 1024], P('fsdp', 'ctx'), may hold values from -0.125 to 0.125
- q_gain: float32 [128], replicated, may hold values from 0.5 to 5
- k_gain: float32 [128], replicated, may hold values from 0.5 to 5
- lengths: int32 [16, 4], replicated, may hold values from 1 to 1024, 2048 in all within a row
- piece_map: int32 [16, 8], replicated, may hold values from 0 to 7, each once within a row
- owner: int32 [8, 16, 256], P('ctx', 'fsdp'), may hold values from 0 to 127, as said below
- slot: int32 [8, 16, 256], P('ctx', 'fsdp'), may hold values from 0 to 511, as said below
Outputs:
- attended: bfloat16 [8, 16, 256, 2048], P('ctx', 'fsdp')
- cache: bfloat16 [65536, 2048], P(('ctx', 'fsdp'))
The draws below stay inside these ranges and needn't reach their ends.
Inputs may be any that keep to these rules, and one draw needn't show every extreme that they name: `lengths`: each row sums to 2048; its largest entry is 1024. `piece_map`: each row holds every piece once. At most 4 tokens of one device go to one owner; in every draw one owner receives exactly 4 from every device. `slot`: tokens with the same owner have distinct slots.
All inputs are finite; a program needn't handle non-finite values.
Results may differ from the reference program's by a relative error of at most 0.0035.
The reference program's roundings to bfloat16 on the way count: a program that leaves them out, or rounds other values in their place, can miss the bound.
Values may be sent and summed in bfloat16 or wider, within the bound.
No kernel may reach another device: no remote copies, remote signals or barrier semaphores. Data moves between devices by JAX's collectives and lax.ppermute only.
A program may use at most 128 MiB of HBM per device.

```python
import math
import jax
import jax.numpy as jnp
import numpy as np
from jax import lax

MODEL_WIDTH = 2048
QUERY_HEADS = 16
KEY_VALUE_HEADS = 8
HEAD_WIDTH = 128
TOK_DEV = 256
NSEG = 4
QW = 2048
KW = 1024
PIECES = 8
GROUPS = 16
STREAM_TOKENS = 2048
LONGEST = 1024
OWNERS = 128
MOST = 4
CAP = 512


def route_tables(key):
    base_key = jax.random.fold_in(key, 11)
    heavy_key, source_key, table_key = jax.random.split(base_key, 3)
    heavy_owner = jax.random.randint(heavy_key, (), 0, OWNERS)

    def one_source(sub_key):
        first_key, second_key, third_key = jax.random.split(sub_key, 3)
        spread = jax.random.permutation(first_key, (OWNERS - 1) * MOST)[:TOK_DEV - MOST]
        other_owner = (heavy_owner + 1 + spread // MOST) % OWNERS
        other_rank = spread % MOST
        heavy_rank = jax.random.permutation(second_key, MOST)
        owner_list = jnp.concatenate([jnp.full((MOST,), heavy_owner, jnp.int32), other_owner.astype(jnp.int32)])
        rank_list = jnp.concatenate([heavy_rank.astype(jnp.int32), other_rank.astype(jnp.int32)])
        shuffle = jax.random.permutation(third_key, TOK_DEV)
        return (owner_list[shuffle], rank_list[shuffle])
    owners, rank_list = jax.vmap(one_source)(jax.random.split(source_key, OWNERS))
    tables = jax.vmap(lambda sub_key: jax.random.permutation(sub_key, CAP).astype(jnp.int32))(jax.random.split(table_key, OWNERS))
    sources = jnp.arange(OWNERS, dtype=jnp.int32)[:, None]
    slot_ids = tables[owners, sources * MOST + rank_list]
    return (owners.reshape(PIECES, GROUPS, TOK_DEV), slot_ids.astype(jnp.int32).reshape(PIECES, GROUPS, TOK_DEV))


def draw_owner(key, part):
    return route_tables(key)[0]


def draw_slot(key, part):
    return route_tables(key)[1]


def projection_tables(key):
    base_key = jax.random.fold_in(key, 17)
    query_key, jitter_seed = jax.random.split(base_key, 2)
    query_matrix = jnp.clip(0.4 * jax.random.normal(query_key, (MODEL_WIDTH, QW), jnp.float32), -1.0, 1.0)
    key_table = jnp.clip(0.4 * jax.random.normal(jitter_seed, (MODEL_WIDTH, KW), jnp.float32), -1.0, 1.0)
    return (query_matrix, key_table)


def draw_w_query(key, part):
    return projection_tables(key)[0].astype(jnp.bfloat16)


def draw_w_key(key, part):
    return projection_tables(key)[1].astype(jnp.bfloat16)


def draw_hidden(key, part):
    sub_key = jax.random.fold_in(key, 7)
    first_key = jax.random.fold_in(sub_key, 0)
    full_shape = (PIECES, GROUPS, TOK_DEV, MODEL_WIDTH)
    values = jnp.clip(jax.random.normal(first_key, full_shape, jnp.float32), -4.5, 4.5)
    return values.astype(jnp.bfloat16)


def draw_q_gain(key, part):
    sub_key = jax.random.fold_in(key, 3)
    return jax.random.uniform(sub_key, (HEAD_WIDTH,), jnp.float32, 0.5, 2.0)


def draw_k_gain(key, part):
    sub_key = jax.random.fold_in(key, 5)
    return jax.random.uniform(sub_key, (HEAD_WIDTH,), jnp.float32, 0.5, 2.0)


def block_scale(stream_key, dims, cuts, least, top_value):
    level, own = 1.0, jax.random.fold_in(stream_key, 6)
    for dim, parts in cuts:
        draws = jnp.exp(jax.random.uniform(jax.random.fold_in(own, dim), (parts,), jnp.float32, least / len(cuts), top_value / len(cuts)))
        level = level * jnp.repeat(draws, dims[dim] // parts).reshape([-1 if axis == dim else 1 for axis in range(len(dims))])
    return level


def profile(count, total, most, skew):
    portions = [(1 << 20) // math.isqrt(grade ** skew) + 1 for grade in range(2, count + 1)]
    spare, given = total - most - (count - 1), [1] * (count - 1)
    while spare > 0:
        candidates = [i for i in range(count - 1) if given[i] < most]
        mass, left = sum([portions[i] for i in candidates]), spare
        for i in candidates:
            more = min(most - given[i], max(1, left * portions[i] // mass), spare)
            given[i] = given[i] + more
            spare = spare - more
    return np.array([most] + given)


def uneven_parts(own_key, number_of, total, bound, slope):
    if number_of == 2:
        one = jax.random.randint(own_key, (), max(1, total - bound), min(bound, total - 1) + 1)
        return jnp.stack([one, total - one])
    sizes = jnp.asarray(profile(number_of, total, bound, slope), jnp.int32)
    pairs = (number_of - 1) // 2
    source_of, taker = sizes[1:1 + 2 * pairs:2], sizes[2:2 + 2 * pairs:2]
    room = jnp.minimum(source_of - 1, bound - taker)
    shifted = jax.random.randint(jax.random.fold_in(own_key, 1), (pairs,), 0, 1 << 20) % (room + 1)
    sizes = sizes.at[1:1 + 2 * pairs:2].set(source_of - shifted).at[2:2 + 2 * pairs:2].set(taker + shifted)
    return sizes[jax.random.permutation(jax.random.fold_in(own_key, 2), number_of)]


def bell_draw(rng, shape, scale, most, cuts=(), kind=jnp.bfloat16):
    drawn = scale * jax.random.normal(rng, shape, jnp.float32)
    if cuts:
        drawn = drawn * block_scale(rng, shape, cuts, -0.22, 0.18)
    return jnp.clip(drawn, -most, most).astype(kind)


def setup_inputs(seed: int = 0) -> dict:
    splits = jax.random.split(jax.random.key(seed), 12)
    hidden = draw_hidden(jax.random.fold_in(splits[11], 71), 0)
    norm_gain = jnp.clip(1.0 + 0.18 * jax.random.normal(splits[1], (MODEL_WIDTH,), jnp.float32), 0.1, 1.9)
    w_query = draw_w_query(jax.random.fold_in(splits[11], 71), 0)
    w_key = draw_w_key(jax.random.fold_in(splits[11], 71), 0)
    w_value = bell_draw(splits[4], (MODEL_WIDTH, KW), MODEL_WIDTH ** -0.5, 0.125, ((0, 16), (1, 8)))
    q_gain = draw_q_gain(jax.random.fold_in(splits[11], 71), 0)
    k_gain = draw_k_gain(jax.random.fold_in(splits[11], 71), 0)
    lengths = jax.vmap(lambda own: uneven_parts(own, NSEG, STREAM_TOKENS, LONGEST, 2))(jax.random.split(splits[7], GROUPS)).reshape((GROUPS, NSEG)).astype(jnp.int32)
    piece_map = jax.vmap(lambda own: jax.random.permutation(own, PIECES))(jax.random.split(splits[8], GROUPS)).reshape((GROUPS, PIECES)).astype(jnp.int32)
    owner = draw_owner(jax.random.fold_in(splits[11], 71), 0)
    slot = draw_slot(jax.random.fold_in(splits[11], 71), 0)
    return {"hidden": hidden, "norm_gain": norm_gain, "w_query": w_query, "w_key": w_key, "w_value": w_value, "q_gain": q_gain, "k_gain": k_gain, "lengths": lengths, "piece_map": piece_map, "owner": owner, "slot": slot}


EPSILON = 1e-06
THETA = 1000000.0
NEG_BIG = -1e+30

def norm_rope(projected, gain_vec, relative, head_size):
    row_count = projected.shape[0]
    head_count = projected.shape[1] // head_size
    shaped = projected.reshape(row_count, head_count, head_size)
    factor = lax.rsqrt(lax.optimization_barrier(jnp.mean(shaped * shaped, axis=-1, keepdims=True)) + EPSILON)
    normal = shaped * factor * gain_vec
    half_size = head_size // 2
    frequency = jnp.exp(jnp.arange(half_size, dtype=jnp.float32) * (-2.0 * math.log(THETA) / head_size))
    angles = relative.astype(jnp.float32)[:, None] * frequency[None, :]
    cosine = jnp.cos(angles)[:, None, :]
    sine_part = jnp.sin(angles)[:, None, :]
    first_half = normal[..., :half_size]
    second = normal[..., half_size:]
    turned = jnp.concatenate([first_half * cosine - second * sine_part, second * cosine + first_half * sine_part], axis=-1)
    return turned.reshape(row_count, head_count * head_size).astype(jnp.bfloat16)

def reference(hidden, norm_gain, w_query, w_key, w_value, q_gain, k_gain, lengths, piece_map, owner, slot):
    inputs = hidden.astype(jnp.float32)
    factor = lax.rsqrt(lax.optimization_barrier(jnp.mean(inputs * inputs, axis=-1, keepdims=True)) + EPSILON)
    normed = (inputs * factor * norm_gain).astype(jnp.bfloat16)
    flat_rows = normed.reshape(-1, MODEL_WIDTH)
    query_raw = jnp.dot(flat_rows, w_query, preferred_element_type=jnp.float32)
    key_raw = jnp.dot(flat_rows, w_key, preferred_element_type=jnp.float32)
    value_rows = jnp.dot(flat_rows, w_value, preferred_element_type=jnp.float32).astype(jnp.bfloat16)
    pieces = jnp.transpose(piece_map).astype(jnp.int32)
    positions = pieces[:, :, None] * TOK_DEV + jnp.arange(TOK_DEV, dtype=jnp.int32)[None, None, :]
    seg_ends = jnp.cumsum(lengths, axis=1, dtype=jnp.int32)
    starts = seg_ends - lengths
    segment = lax.optimization_barrier(jnp.sum((positions[..., None] >= seg_ends[None, :, None, :]).astype(jnp.int32), axis=-1, dtype=jnp.int32))
    seg_ids = jnp.arange(NSEG, dtype=jnp.int32)
    relative = positions - lax.optimization_barrier(jnp.sum(jnp.where(segment[..., None] == seg_ids, starts[None, :, None, :], 0), axis=-1, dtype=jnp.int32))
    query_rows = norm_rope(query_raw, q_gain, relative.reshape(-1), HEAD_WIDTH)
    key_rows = norm_rope(key_raw, k_gain, relative.reshape(-1), HEAD_WIDTH)
    cache_index = (owner.reshape(-1) * CAP + slot.reshape(-1)).astype(jnp.int32)
    cache = jnp.zeros((OWNERS * CAP, 2 * KW), jnp.bfloat16).at[cache_index].set(jnp.concatenate([key_rows, value_rows], axis=1))

    def by_group(array, width):
        return jnp.swapaxes(array.reshape(PIECES, GROUPS, TOK_DEV, width), 0, 1).reshape(GROUPS, STREAM_TOKENS, width)
    group_pos = jnp.swapaxes(positions, 0, 1).reshape(GROUPS, STREAM_TOKENS)
    group_seg = jnp.swapaxes(segment, 0, 1).reshape(GROUPS, STREAM_TOKENS)
    rows_per_block = 512 if STREAM_TOKENS % 512 == 0 else STREAM_TOKENS
    group_width = QUERY_HEADS // KEY_VALUE_HEADS
    scale_factor = 1.0 / math.sqrt(HEAD_WIDTH)

    def one_group(operands):
        query_group, grouped_keys, grouped_values, pos_group, seg_group = operands
        heads_of_key = grouped_keys.reshape(STREAM_TOKENS, KEY_VALUE_HEADS, HEAD_WIDTH).astype(jnp.float32)
        heads_of_value = grouped_values.reshape(STREAM_TOKENS, KEY_VALUE_HEADS, HEAD_WIDTH).astype(jnp.float32)

        def one_block(block_in):
            block_of_query, pos_block, seg_block = block_in
            heads_of_query = block_of_query.reshape(rows_per_block, KEY_VALUE_HEADS, group_width, HEAD_WIDTH).astype(jnp.float32)
            scores = jnp.einsum('tkgd,skd->tkgs', heads_of_query, heads_of_key) * scale_factor
            visible = (seg_block[:, None] == seg_group[None, :]) & (pos_group[None, :] <= pos_block[:, None])
            visible = visible[:, None, None, :]
            masked = jnp.where(visible, scores, NEG_BIG)
            row_max = lax.optimization_barrier(jnp.max(masked, axis=-1, keepdims=True))
            weights = jnp.where(visible, jnp.exp(masked - row_max), 0.0)
            row_sum = lax.optimization_barrier(jnp.sum(weights, axis=-1))
            rounded = weights.astype(jnp.bfloat16).astype(jnp.float32)
            mixed = jnp.einsum('tkgs,skd->tkgd', rounded, heads_of_value) / row_sum[..., None]
            return mixed.reshape(rows_per_block, QW).astype(jnp.bfloat16)
        return lax.map(one_block, (query_group.reshape(-1, rows_per_block, QW), pos_group.reshape(-1, rows_per_block), seg_group.reshape(-1, rows_per_block)))
    outputs = lax.map(one_group, (by_group(query_rows, QW), by_group(key_rows, KW), by_group(value_rows, KW), group_pos, group_seg))
    attended = jnp.swapaxes(outputs.reshape(GROUPS, PIECES, TOK_DEV, QW), 0, 1)
    return (attended, cache)
```

```python
import math

import jax
import jax.numpy as jnp
from jax import lax
from jax.experimental import pallas as pl
from jax.experimental.pallas import tpu as pltpu
from jax.sharding import Mesh, PartitionSpec as P

HEAD = 128
TOK = 256
EPSILON = 1e-06
THETA = 1000000.0
NEG_BIG = -1e30
MOST = 4
MIB = 1 << 20
ROUTE = 8
CTX = ("y", "core")
FSDP = ("x", "z")


def shift(value, axis, by):
    size = lax.axis_size(axis)
    return lax.ppermute(value, axis, [(i, (i + by) % size) for i in range(size)])


def norm_rope(raw, gain, cos, sin):
    factor = lax.rsqrt(jnp.mean(raw * raw, axis=-1, keepdims=True) + EPSILON)
    normal = raw * factor * gain
    return (normal * cos + pltpu.roll(normal, HEAD // 2, 1) * sin).astype(jnp.bfloat16)


def call(kernel, out_shape, specs, outs, mib, cost, name, scratch=(), grid=(), maps=()):
    flops, moved = cost
    return pl.pallas_call(
        kernel,
        grid_spec=pltpu.PrefetchScalarGridSpec(
            num_scalar_prefetch=len(maps),
            grid=grid,
            in_specs=specs,
            out_specs=outs,
            scratch_shapes=scratch,
        ),
        out_shape=out_shape,
        compiler_params=pltpu.CompilerParams(vmem_limit_bytes=mib * MIB),
        cost_estimate=pl.CostEstimate(flops=flops, bytes_accessed=moved * MIB, transcendentals=0),
        name=name,
    )


def shape(*dims, dtype=jnp.bfloat16):
    return jax.ShapeDtypeStruct(dims, dtype)


WHOLE = pl.BlockSpec(memory_space=pltpu.VMEM)
FAR = pl.BlockSpec(memory_space=pltpu.HBM)


def pack_kernel(hidden, routes, out, sem):
    move = pltpu.make_async_copy(hidden, out.at[pl.ds(ROUTE, TOK)], sem)
    move.start()
    out[0:ROUTE, :] = jnp.zeros((ROUTE, out.shape[1]), out.dtype)
    out[0:1, 0:TOK] = routes[...].astype(out.dtype)
    move.wait()


def pack(hidden, routes):
    return call(
        pack_kernel,
        shape(ROUTE + TOK, 2048),
        [FAR, WHOLE],
        WHOLE,
        4,
        (0, 2),
        "pack",
        [pltpu.SemaphoreType.DMA],
    )(hidden, routes)


def spread_weights_kernel(a, b, c, routes, out, part, sems):
    moves = [
        pltpu.make_async_copy(a, part.at[:, pl.ds(0, 2 * HEAD)], sems.at[0]),
        pltpu.make_async_copy(b, part.at[:, pl.ds(2 * HEAD, HEAD)], sems.at[1]),
        pltpu.make_async_copy(c, part.at[:, pl.ds(3 * HEAD, HEAD)], sems.at[2]),
    ]
    for move in moves:
        move.start()
    for i in range(16):
        out[i, 0:ROUTE, 0:HEAD] = routes[i]
        out[i, 0:ROUTE, HEAD:] = jnp.zeros((ROUTE, 3 * HEAD), out.dtype)
    for move in moves:
        move.wait()
    for i in range(16):
        out[i, ROUTE:, :] = part[...]


def spread_weights(a, b, c, routes):
    return call(
        spread_weights_kernel,
        shape(16, ROUTE + 128, 4 * HEAD),
        [FAR, FAR, FAR, WHOLE],
        WHOLE,
        6,
        (0, 3),
        "spread_weights",
        [pltpu.VMEM((128, 4 * HEAD), jnp.bfloat16), pltpu.SemaphoreType.DMA((3,))],
    )(a, b, c, routes)


def join_kernel(got, w_q, w_kv, routes):
    for i in range(16):
        w_q[i * 128 : (i + 1) * 128, :] = got[i, ROUTE:, 0 : 2 * HEAD]
        w_kv[i * 128 : (i + 1) * 128, :] = got[i, ROUTE:, 2 * HEAD :]
        routes[i] = got[i, 0:ROUTE, 0:HEAD]


def join_weights(got):
    return call(
        join_kernel,
        [shape(2048, 2 * HEAD), shape(2048, 2 * HEAD), shape(16, ROUTE, HEAD)],
        [WHOLE],
        [WHOLE] * 3,
        6,
        (0, 4),
        "join_weights",
    )(got)


def owner_row(ref):
    own = ref[0:ROUTE, 0:TOK].astype(jnp.float32)
    column = jnp.transpose(own)[:, 0:1]
    row = own[0:1]
    token = lax.broadcasted_iota(jnp.int32, (TOK, TOK), 0)
    other = lax.broadcasted_iota(jnp.int32, (TOK, TOK), 1)
    same = (column == row) & (token < other)
    rank = jnp.sum(same.astype(jnp.float32), axis=0, keepdims=True)
    return (row * 8 + rank).astype(jnp.int32)


def normalize(pairs, core, gain):
    count = sum(len(p) for p in pairs)

    def kernel(core_ref, *refs):
        gain_ref, out, codes = refs[count:]
        at = 0
        for i, p in enumerate(pairs):
            row, side = 0, 0
            for source in refs[at : at + len(p)]:
                start = source.shape[0] % 16
                if start:
                    mine = core_ref[0] + side - 2 * core_ref[0] * side
                    codes[i, :, side * TOK : (side + 1) * TOK] = owner_row(source) + mine * MOST
                    side += 1
                for j in range(start, source.shape[0], 128):
                    x = source[j : j + 128, :].astype(jnp.float32)
                    factor = lax.rsqrt(jnp.mean(x * x, axis=-1, keepdims=True) + EPSILON)
                    out[i, row : row + 128, :] = (x * factor * gain_ref[...]).astype(jnp.bfloat16)
                    row += 128
            at += len(p)

    n = len(pairs)
    return call(
        kernel,
        [shape(n, 2 * TOK, 2048), shape(n, 1, 2 * TOK, dtype=jnp.int32)],
        [pl.BlockSpec(memory_space=pltpu.SMEM)] + [WHOLE] * (count + 1),
        [WHOLE] * 2,
        18,
        (8 * n * MIB, 4 * n),
        "normalize",
    )(core, *(x for p in pairs for x in p), gain)


def keys_kernel(
    ys, piece_of, x_a, x_b, code_a, code_b, w, gain, cos, sin, k_out, v_out, b_out, kv
):
    pair = pl.program_id(0)

    def go(x, code):
        raw = jnp.dot(x, w[...], preferred_element_type=jnp.float32)
        key = norm_rope(raw[:, :HEAD], gain[...], cos[0], sin[0])
        value = raw[:, HEAD:].astype(jnp.bfloat16)
        for side in range(2):
            at = pl.multiple_of(piece_of[2 * pair + side] * TOK, TOK)
            k_out[pl.ds(at, TOK), :] = key[side * TOK : (side + 1) * TOK]
            v_out[pl.ds(at, TOK), :] = value[side * TOK : (side + 1) * TOK]
        kv[:, :HEAD] = key
        kv[:, HEAD:] = value
        place = lax.broadcasted_iota(jnp.int32, (8 * 128, 2 * TOK), 0)
        pick = (place == code).astype(jnp.bfloat16)
        got = jnp.dot(pick, kv[...], preferred_element_type=jnp.float32)
        b_out[...] = got.reshape(128, 8, 2 * HEAD).astype(jnp.bfloat16)

    pl.when(pair < 3)(lambda: go(x_a[jnp.minimum(pair, 2)], code_a[jnp.minimum(pair, 2)]))
    pl.when(pair == 3)(lambda: go(x_b[0], code_b[0]))


def keys(y_of_pair, piece_of, x_a, x_b, code_a, code_b, w, gain, cos, sin):
    maps = y_of_pair, piece_of
    table = pl.BlockSpec((1, 2 * TOK, HEAD), lambda i, *_: (i, 0, 0))
    stream = pl.BlockSpec((8 * TOK, HEAD), lambda i, *_: (0, 0))
    return call(
        keys_kernel,
        [shape(8 * TOK, HEAD), shape(8 * TOK, HEAD), shape(128, 32, 2 * HEAD)],
        [WHOLE] * 6 + [table] * 2,
        [stream, stream, pl.BlockSpec((128, 8, 2 * HEAD), lambda i, ys, _: (0, ys[i], 0))],
        12,
        (2 * 2048 * 2048 * 256, 12),
        "keys",
        [pltpu.VMEM((2 * TOK, 2 * HEAD), jnp.bfloat16)],
        (4,),
        maps,
    )(*maps, x_a, x_b, code_a, code_b, w, gain, cos, sin)


def queries_kernel(x_a, x_b, w, gain, cos, sin, out):
    pair = pl.program_id(0)

    def go(x):
        raw = jnp.dot(x, w[...], preferred_element_type=jnp.float32)
        for h in range(2):
            part = slice(h * HEAD, (h + 1) * HEAD)
            out[0, :, part] = norm_rope(raw[:, part], gain[...], cos[0], sin[0])

    pl.when(pair < 3)(lambda: go(x_a[jnp.minimum(pair, 2)]))
    pl.when(pair == 3)(lambda: go(x_b[0]))


def queries(x_a, x_b, w, gain, cos, sin):
    table = pl.BlockSpec((1, 2 * TOK, HEAD), lambda i: (i, 0, 0))
    return call(
        queries_kernel,
        shape(4, 2 * TOK, 2 * HEAD),
        [WHOLE] * 4 + [table] * 2,
        pl.BlockSpec((1, 2 * TOK, 2 * HEAD), lambda i: (i, 0, 0)),
        12,
        (2 * 2048 * 2048 * 256, 12),
        "queries",
        (),
        (4,),
    )(x_a, x_b, w, gain, cos, sin)


def attend_kernel(piece_of, ctx_of, low, starts, q, keys, values, lead, out):
    p = piece_of[pl.program_id(0)]
    lo = low[p]
    out[0, 0:ROUTE, :] = lead[0]
    both = jnp.concatenate([q[0, :, :HEAD], q[0, :, HEAD:]], axis=0)
    place = p * TOK + jnp.bitwise_and(lax.broadcasted_iota(jnp.int32, (2 * TOK, 1), 0), TOK - 1)
    begin = jnp.zeros_like(place)
    for n in range(1, 4):
        begin = jnp.where(starts[n] <= place, starts[n], begin)

    def blocks(count):
        at = pl.multiple_of(lo * TOK, TOK)
        span = count * TOK
        s = lax.dot_general(
            both,
            keys[pl.ds(at, span), :],
            (((1,), (1,)), ((), ())),
            preferred_element_type=jnp.float32,
        )
        spot = at + lax.broadcasted_iota(jnp.int32, (1, span), 1)
        s = jnp.where((spot <= place) & (spot >= begin), s, NEG_BIG)
        top = jnp.max(s, axis=1, keepdims=True)
        e = jnp.exp((s - top) * (1.0 / math.sqrt(HEAD)))
        total = jnp.sum(e, axis=1, keepdims=True)
        mixed = jnp.dot(
            e.astype(jnp.bfloat16), values[pl.ds(at, span), :], preferred_element_type=jnp.float32
        )
        mixed = (mixed / total).astype(jnp.bfloat16)
        out[0, ROUTE:, :HEAD] = mixed[:TOK]
        out[0, ROUTE:, HEAD:] = mixed[TOK:]

    for count in range(1, 6):
        pl.when(p + 1 - lo == count)(lambda count=count: blocks(count))


def attend(piece_of, ctx_of, low, starts, q, k, v, leads):
    maps = piece_of, ctx_of, low, starts
    return call(
        attend_kernel,
        shape(8, ROUTE + TOK, 2 * HEAD),
        [
            pl.BlockSpec((1, TOK, 2 * HEAD), lambda i, *_: (i, 0, 0)),
            WHOLE,
            WHOLE,
            pl.BlockSpec((1, ROUTE, 2 * HEAD), lambda i, p, c, *_: (c[i], 0, 0)),
        ],
        pl.BlockSpec((1, ROUTE + TOK, 2 * HEAD), lambda i, *_: (i, 0, 0)),
        14,
        (8 * 2048 * 2048 * 128, 4),
        "attend",
        (),
        (8,),
        maps,
    )(*maps, q.reshape(8, TOK, 2 * HEAD), k, v, leads)


def cache_kernel(slots, got, out):
    rows = lax.broadcasted_iota(jnp.int32, (512, 512), 0)
    pick = (rows == slots[...]).astype(jnp.bfloat16)
    for c in range(8):
        put = jnp.dot(pick, got[c], preferred_element_type=jnp.float32).astype(jnp.bfloat16)
        out[:, c * HEAD : (c + 1) * HEAD] = put[:, :HEAD]
        out[:, (8 + c) * HEAD : (9 + c) * HEAD] = put[:, HEAD:]


def fill_cache(slots, got):
    whole = pl.BlockSpec(memory_space=pltpu.VMEM)
    return pl.pallas_call(
        cache_kernel,
        out_shape=jax.ShapeDtypeStruct((512, 2048), jnp.bfloat16),
        in_specs=[whole, whole],
        out_specs=whole,
        compiler_params=pltpu.CompilerParams(vmem_limit_bytes=32 * MIB),
        cost_estimate=pl.CostEstimate(
            flops=2 * 512 * 512 * 2048, bytes_accessed=4 * MIB, transcendentals=0
        ),
        name="fill_cache",
    )(slots, got)


def spread_kernel(ctx_of, *refs):
    out, leads = refs[-2:]
    side = 0
    for ref in refs[:-2]:
        for i in range(ref.shape[0]):
            ctx = ctx_of[side]
            out[:, pl.ds(pl.multiple_of(ctx * 2 * HEAD, 2 * HEAD), 2 * HEAD)] = ref[i, ROUTE:]
            leads[ctx] = ref[i, 0:ROUTE, 0:HEAD].astype(jnp.float32)
            side += 1


def spread(ctx_of, parts):
    return call(
        spread_kernel,
        [shape(TOK, 2048), shape(8, ROUTE, HEAD, dtype=jnp.float32)],
        [pl.BlockSpec(memory_space=pltpu.SMEM)] + [WHOLE] * len(parts),
        [WHOLE] * 2,
        6,
        (0, 2),
        "spread",
    )(ctx_of, *parts)


def choose(index, table):
    hit = index[:, None] == jnp.arange(table.shape[0], dtype=jnp.int32)[None, :]
    return jnp.sum(jnp.where(hit, table[None], 0), axis=1, dtype=jnp.int32)


def ring(value, axis, half):
    below, above = shift(value, axis, 1), shift(value, axis, -1)
    return [value, above, below, shift(above[:half], axis, -1), shift(below[half:], axis, 1)]


def shards(
    hidden, norm_gain, w_query, w_key, w_value, q_gain, k_gain, lengths, piece_map, owner, slot
):
    y, core = lax.axis_index("y"), lax.axis_index("core")
    group = lax.axis_index(FSDP)
    own = owner[0, 0]
    offsets = jnp.array([0, 1, 3, 2], jnp.int32)

    h = pack(hidden[0, 0], own[None])
    near, above, below, far_lo, far_hi = ring(h, "y", ROUTE + TOK // 2)
    swap = lambda value: shift(value, "core", 1)
    pairs = [
        (near, swap(near)),
        (above, swap(above)),
        (below, swap(below)),
        (far_lo, far_hi, swap(far_lo), swap(far_hi)),
    ]

    token = jnp.arange(TOK, dtype=jnp.int32)
    same = (own[:, None] == own[None, :]) & (token[None, :] < token[:, None])
    rank = jnp.sum(same.astype(jnp.int32), axis=1, dtype=jnp.int32)
    spot = (own % 16) * 32 + (own // 16) * MOST + rank
    hit = spot[None, :] == jnp.arange(512, dtype=jnp.int32)[:, None]
    table = jnp.sum(jnp.where(hit, slot[0, 0][None, :] + 1, 0), axis=1, dtype=jnp.int32)
    table = table.reshape(16, 1, 32)
    table = jnp.concatenate([table // 16, table % 16], axis=1).astype(jnp.bfloat16)
    table = jnp.pad(table, ((0, 0), (0, ROUTE - 2), (0, HEAD - 32)))
    _, table = lax.optimization_barrier((h, table))
    w = spread_weights(w_query, w_key, w_value, table)
    w = lax.all_to_all(w, FSDP, split_axis=0, concat_axis=0, tiled=True)
    w_q, w_kv, leads = join_weights(w)
    leads = leads[:, :2, :32].reshape(16, 2, 8, MOST).transpose(2, 1, 0, 3).reshape(8, 2, 64)
    leads = jnp.pad(leads, ((0, 0), (0, ROUTE - 2), (0, 2 * HEAD - 64)))

    my_pieces = lax.dynamic_index_in_dim(piece_map, group, 0, keepdims=False)
    my_lengths = lax.dynamic_index_in_dim(lengths, group, 0, keepdims=False)
    ends = jnp.cumsum(my_lengths, dtype=jnp.int32)
    starts = ends - my_lengths
    y_of_pair = ((y + offsets) % 4).astype(jnp.int32)
    core_of = jnp.stack([core, 1 - core]).astype(jnp.int32)
    ctx_of_slot = (y_of_pair[:, None] * 2 + core_of[None, :]).reshape(-1)
    piece_of_slot = choose(ctx_of_slot, my_pieces)
    eight = jnp.arange(8, dtype=jnp.int32)

    def begin_of(places):
        reached = starts[None, :] <= places.reshape(-1, 1)
        return jnp.max(jnp.where(reached, starts[None, :], 0), axis=1).reshape(places.shape)

    low = begin_of(eight * TOK) // TOK
    places = piece_of_slot[:, None] * TOK + jnp.arange(TOK, dtype=jnp.int32)[None, :]
    relative = places - begin_of(places)
    half = HEAD // 2
    frequency = jnp.exp(jnp.arange(half, dtype=jnp.float32) * (-2.0 * math.log(THETA) / HEAD))
    angles = relative.astype(jnp.float32).reshape(4, 2 * TOK, 1) * frequency
    cos, sin = jnp.cos(angles), jnp.sin(angles)
    cos = jnp.concatenate([cos, cos], axis=-1)
    sin = jnp.concatenate([-sin, sin], axis=-1)

    core = core.astype(jnp.int32)[None]
    x_a, code_a = normalize(pairs[:3], core, norm_gain[None])
    x_b, code_b = normalize(pairs[3:], core, norm_gain[None])
    k, v, buckets = keys(
        y_of_pair, piece_of_slot, x_a, x_b, code_a, code_b, w_kv, k_gain[None], cos, sin
    )
    buckets, x_a = lax.optimization_barrier((buckets, x_a))
    got = lax.all_to_all(buckets, CTX + FSDP, split_axis=0, concat_axis=0, tiled=True)
    q = queries(x_a, x_b, w_q, q_gain[None], cos, sin)
    mixed = attend(piece_of_slot, ctx_of_slot, low, starts, q, k, v, leads)
    mixed = mixed.reshape(4, 2, ROUTE + TOK, 2 * HEAD)
    from_above = shift(mixed[2:], "y", -1)
    from_below = shift(mixed[1], "y", 1)
    from_far = shift(from_above[1], "y", -1)
    mine = [mixed[0], from_above[0], from_below, from_far]
    other = [swap(m[1]) for m in mine]
    parts = [p for m, o in zip(mine, other) for p in (m[0][None], o[None])]
    attended, leads = spread(ctx_of_slot, parts)
    table = (leads[:, 0] * 16 + leads[:, 1]).astype(jnp.int32)[:, :64] - 1
    table = table.reshape(8, 16, MOST).transpose(1, 0, 2).reshape(1, 512)
    cache = fill_cache(table, got.reshape(8, 512, 2 * HEAD))
    return attended[None, None], cache


def solution(mesh):
    split = Mesh(mesh.devices.reshape(4, 2, 4, 4), (*CTX, *FSDP))
    placed = (
        P(CTX, FSDP, None, None),
        P(),
        P(FSDP, CTX),
        P(FSDP, CTX),
        P(FSDP, CTX),
        P(),
        P(),
        P(),
        P(),
        P(CTX, FSDP, None),
        P(CTX, FSDP, None),
    )
    return jax.shard_map(
        shards,
        mesh=split,
        in_specs=placed,
        out_specs=(P(CTX, FSDP, None, None), P((*CTX, *FSDP), None)),
        check_vma=False,
    )
```

```python
import math

import jax
import jax.numpy as jnp
from jax import lax
from jax.experimental import pallas as pl
from jax.experimental.pallas import tpu as pltpu
from jax.sharding import Mesh, PartitionSpec as P

HEAD = 128
TOK = 256
EPSILON = 1e-06
THETA = 1000000.0
NEG_BIG = -1e30
MOST = 4
MIB = 1 << 20
ROUTE = 8
CTX = ("y", "core")
FSDP = ("x", "z")


def shift(value, axis, by):
    size = lax.axis_size(axis)
    return lax.ppermute(value, axis, [(i, (i + by) % size) for i in range(size)])


def norm_rope(raw, gain, cos, sin):
    factor = lax.rsqrt(jnp.mean(raw * raw, axis=-1, keepdims=True) + EPSILON)
    normal = raw * factor * gain
    return (normal * cos + pltpu.roll(normal, HEAD // 2, 1) * sin).astype(jnp.bfloat16)


def call(kernel, out_shape, specs, outs, mib, cost, name, scratch=(), grid=(), maps=()):
    flops, moved = cost
    return pl.pallas_call(
        kernel,
        grid_spec=pltpu.PrefetchScalarGridSpec(
            num_scalar_prefetch=len(maps),
            grid=grid,
            in_specs=specs,
            out_specs=outs,
            scratch_shapes=scratch,
        ),
        out_shape=out_shape,
        compiler_params=pltpu.CompilerParams(vmem_limit_bytes=mib * MIB),
        cost_estimate=pl.CostEstimate(flops=flops, bytes_accessed=moved * MIB, transcendentals=0),
        name=name,
    )


def shape(*dims, dtype=jnp.bfloat16):
    return jax.ShapeDtypeStruct(dims, dtype)


WHOLE = pl.BlockSpec(memory_space=pltpu.VMEM)
FAR = pl.BlockSpec(memory_space=pltpu.HBM)


def pack_kernel(hidden, own_hbm, gain_hbm, out, x, own, gain, sems):
    first = pltpu.make_async_copy(own_hbm, own, sems.at[0])
    move = pltpu.make_async_copy(hidden, x, sems.at[1])
    last = pltpu.make_async_copy(gain_hbm, gain, sems.at[2])
    first.start()
    move.start()
    last.start()
    first.wait()
    row = own[...].astype(jnp.float32)
    column = jnp.transpose(jnp.broadcast_to(row, (ROUTE, TOK)))[:, 0:1]
    token = lax.broadcasted_iota(jnp.int32, (TOK, TOK), 0)
    other = lax.broadcasted_iota(jnp.int32, (TOK, TOK), 1)
    same = (column == row) & (token < other)
    rank = jnp.sum(same.astype(jnp.float32), axis=0, keepdims=True)
    out[TOK:, :] = jnp.zeros((ROUTE, out.shape[1]), out.dtype)
    which = lax.broadcasted_iota(jnp.int32, (ROUTE, TOK), 0)
    lead = jnp.where(which == 0, row, jnp.where(which == 1, rank, 0.0))
    out[TOK:, 0:TOK] = lead.astype(out.dtype)
    move.wait()
    last.wait()
    for i in range(0, TOK, 128):
        part = x[i : i + 128, :].astype(jnp.float32)
        factor = lax.rsqrt(jnp.mean(part * part, axis=-1, keepdims=True) + EPSILON)
        out[i : i + 128, :] = (part * factor * gain[...]).astype(out.dtype)


def pack(hidden, own, gain):
    return call(
        pack_kernel,
        shape(TOK + ROUTE, 2048),
        [FAR, FAR, FAR],
        WHOLE,
        58,
        (0, 2),
        "pack",
        [
            pltpu.VMEM((TOK, 2048), jnp.bfloat16),
            pltpu.VMEM((1, TOK), jnp.int32),
            pltpu.VMEM((1, 2048), jnp.float32),
            pltpu.SemaphoreType.DMA((3,)),
        ],
    )(hidden, own, gain)


def spread_weights_kernel(a, b, c, routes, out, part, sems):
    moves = [
        pltpu.make_async_copy(a, part.at[:, pl.ds(0, 2 * HEAD)], sems.at[0]),
        pltpu.make_async_copy(b, part.at[:, pl.ds(2 * HEAD, HEAD)], sems.at[1]),
        pltpu.make_async_copy(c, part.at[:, pl.ds(3 * HEAD, HEAD)], sems.at[2]),
    ]
    for move in moves:
        move.start()
    for i in range(16):
        out[i, 128:, 0:HEAD] = routes[i]
        out[i, 128:, HEAD:] = jnp.zeros((ROUTE, 3 * HEAD), out.dtype)
    for move in moves:
        move.wait()
    for i in range(16):
        out[i, 0:128, :] = part[...]


def spread_weights(a, b, c, routes):
    return call(
        spread_weights_kernel,
        shape(16, 128 + ROUTE, 4 * HEAD),
        [FAR, FAR, FAR, WHOLE],
        WHOLE,
        6,
        (0, 3),
        "spread_weights",
        [pltpu.VMEM((128, 4 * HEAD), jnp.bfloat16), pltpu.SemaphoreType.DMA((3,))],
    )(a, b, c, routes)


def data_rows(ref):
    return ref.shape[0] - ref.shape[0] % 16


def take_weights(got, part, out):
    for i in range(16):
        out[i * 128 : (i + 1) * 128, :] = got[i, 0:128, part]


def keys(y_of_pair, piece_of, core, pairs, w, gain, cos, sin):
    count = sum(len(p) for p in pairs)

    def kernel(ys, piece, core_ref, *refs):
        w_ref, gain_ref, cos_ref, sin_ref, k_hbm, v_hbm, b_hbm = refs[count : count + 7]
        w_kv, kv, k_out, v_out, b_out, sems = refs[count + 7 :]
        step = pl.program_id(0)

        def send(i):
            at = pl.multiple_of(ys[i] * 8, 8)
            return pltpu.make_async_copy(b_out.at[i], b_hbm.at[:, pl.ds(at, 8), :], sems.at[i])

        @pl.when(step == 0)
        def _():
            take_weights(w_ref, slice(2 * HEAD, 4 * HEAD), w_kv)

        def go(part):
            at = 0
            codes = []
            for ref in part:
                rows = data_rows(ref)
                raw = jnp.dot(ref[0:rows, :], w_kv[...], preferred_element_type=jnp.float32)
                put = slice(at, at + rows)
                kv[put, :HEAD] = norm_rope(
                    raw[:, :HEAD], gain_ref[...], cos_ref[0, put, :], sin_ref[0, put, :]
                )
                kv[put, HEAD:] = raw[:, HEAD:].astype(jnp.bfloat16)
                if rows < ref.shape[0]:
                    lead = ref[rows:, 0:TOK].astype(jnp.float32)
                    side = len(codes)
                    mine = core_ref[0] + side - 2 * core_ref[0] * side
                    codes.append((lead[0:1] * 8 + lead[1:2]).astype(jnp.int32) + mine * MOST)
                at += rows
            place = lax.broadcasted_iota(jnp.int32, (8 * 128, 2 * TOK), 0)
            pick = (place == jnp.concatenate(codes, axis=1)).astype(jnp.bfloat16)
            got = jnp.dot(pick, kv[...], preferred_element_type=jnp.float32)
            b_out[step] = got.reshape(128, 8, 2 * HEAD).astype(jnp.bfloat16)
            send(step).start()
            for side in range(2):
                to = pl.ds(pl.multiple_of(piece[2 * step + side] * TOK, TOK), TOK)
                k_out[to, :] = kv[side * TOK : (side + 1) * TOK, :HEAD]
                v_out[to, :] = kv[side * TOK : (side + 1) * TOK, HEAD:]

        at = 0
        for i, p in enumerate(pairs):
            pl.when(step == i)(lambda part=refs[at : at + len(p)]: go(part))
            at += len(p)

        @pl.when(step == 3)
        def _():
            last = [
                pltpu.make_async_copy(k_out, k_hbm, sems.at[4]),
                pltpu.make_async_copy(v_out, v_hbm, sems.at[5]),
            ]
            for move in last:
                move.start()
            for i in range(4):
                send(i).wait()
            for move in last:
                move.wait()

    maps = y_of_pair, piece_of, core
    table = pl.BlockSpec((1, 2 * TOK, HEAD), lambda i, *_: (i, 0, 0))
    return call(
        kernel,
        [
            pltpu.HBM((8 * TOK, HEAD), jnp.bfloat16),
            pltpu.HBM((8 * TOK, HEAD), jnp.bfloat16),
            pltpu.HBM((128, 32, 2 * HEAD), jnp.bfloat16),
        ],
        [WHOLE] * (count + 2) + [table] * 2,
        [FAR] * 3,
        14,
        (2 * 2048 * 2048 * 256, 12),
        "keys",
        [
            pltpu.VMEM((2048, 2 * HEAD), jnp.bfloat16),
            pltpu.VMEM((2 * TOK, 2 * HEAD), jnp.bfloat16),
            pltpu.VMEM((8 * TOK, HEAD), jnp.bfloat16),
            pltpu.VMEM((8 * TOK, HEAD), jnp.bfloat16),
            pltpu.VMEM((4, 128, 8, 2 * HEAD), jnp.bfloat16),
            pltpu.SemaphoreType.DMA((6,)),
        ],
        (4,),
        maps,
    )(*maps, *(x for p in pairs for x in p), w, gain, cos, sin)


def attend(first, pieces, piece_of, ctx_of, low, starts, w, gain, cos, sin, k, v, leads):
    count = sum(len(p) for p in pieces)

    def kernel(piece, ctx, lows, begins, *refs):
        w_ref, gain_ref, cos_ref, sin_ref, k_hbm, v_hbm, lead, out = refs[count : count + 8]
        w_q, both, keys_ref, values, sems = refs[count + 8 :]
        step = pl.program_id(0)
        moves = [
            pltpu.make_async_copy(k_hbm, keys_ref, sems.at[0]),
            pltpu.make_async_copy(v_hbm, values, sems.at[1]),
        ]

        @pl.when(step == 0)
        def _():
            for move in moves:
                move.start()
            take_weights(w_ref, slice(0, 2 * HEAD), w_q)

        def query(part):
            at = 0
            for ref in part:
                rows = data_rows(ref)
                raw = jnp.dot(ref[0:rows, :], w_q[...], preferred_element_type=jnp.float32)
                put = slice(at, at + rows)
                for h in range(2):
                    both[h * TOK + at : h * TOK + at + rows, :] = norm_rope(
                        raw[:, h * HEAD : (h + 1) * HEAD],
                        gain_ref[...],
                        cos_ref[0, put, :],
                        sin_ref[0, put, :],
                    )
                at += rows

        at = 0
        for i, p in enumerate(pieces):
            pl.when(step == i)(lambda part=refs[at : at + len(p)]: query(part))
            at += len(p)

        @pl.when(step == 0)
        def _():
            for move in moves:
                move.wait()

        p = piece[first + step]
        lo = lows[p]
        out[0, TOK:, :] = lead[0]
        place = p * TOK + lax.broadcasted_iota(jnp.int32, (TOK, 1), 0)
        begin = jnp.zeros_like(place)
        for n in range(1, 4):
            begin = jnp.where(begins[n] <= place, begins[n], begin)

        def blocks(span):
            at = pl.multiple_of(lo * TOK, TOK)
            spot = at + lax.broadcasted_iota(jnp.int32, (1, span), 1)
            seen = (spot <= place) & (spot >= begin)
            for h in range(2):
                s = lax.dot_general(
                    both[h * TOK : (h + 1) * TOK],
                    keys_ref[pl.ds(at, span), :],
                    (((1,), (1,)), ((), ())),
                    preferred_element_type=jnp.float32,
                )
                s = jnp.where(seen, s, NEG_BIG)
                top = jnp.max(s, axis=1, keepdims=True)
                e = jnp.exp((s - top) * (1.0 / math.sqrt(HEAD)))
                total = jnp.sum(e, axis=1, keepdims=True)
                mixed = jnp.dot(
                    e.astype(jnp.bfloat16),
                    values[pl.ds(at, span), :],
                    preferred_element_type=jnp.float32,
                )
                out[0, 0:TOK, h * HEAD : (h + 1) * HEAD] = (mixed / total).astype(jnp.bfloat16)

        for n in range(1, 6):
            pl.when(p + 1 - lo == n)(lambda n=n: blocks(n * TOK))

    maps = piece_of, ctx_of, low, starts
    n = len(pieces)
    table = pl.BlockSpec((1, TOK, HEAD), lambda i, *_: (first // 2 + i // 2, i % 2, 0))
    return call(
        kernel,
        shape(n, TOK + ROUTE, 2 * HEAD),
        [WHOLE] * (count + 2)
        + [table] * 2
        + [FAR] * 2
        + [pl.BlockSpec((1, ROUTE, 2 * HEAD), lambda i, p, c, *_: (c[first + i], 0, 0))],
        pl.BlockSpec((1, TOK + ROUTE, 2 * HEAD), lambda i, *_: (i, 0, 0)),
        16,
        (n * 2048 * 2048 * 128, 4),
        "attend",
        [
            pltpu.VMEM((2048, 2 * HEAD), jnp.bfloat16),
            pltpu.VMEM((2 * TOK, HEAD), jnp.bfloat16),
            pltpu.VMEM((8 * TOK, HEAD), jnp.bfloat16),
            pltpu.VMEM((8 * TOK, HEAD), jnp.bfloat16),
            pltpu.SemaphoreType.DMA((2,)),
        ],
        (n,),
        maps,
    )(
        *maps,
        *(x for p in pieces for x in p),
        w,
        gain,
        cos,
        sin,
        k,
        v,
        leads,
    )


def cache_kernel(leads, got, out, rows, in_sems):
    takes = [pltpu.make_async_copy(got.at[c], rows.at[c], in_sems.at[c]) for c in range(8)]
    for take in takes:
        take.start()
    column = lax.broadcasted_iota(jnp.int32, (HEAD, 512), 1)
    entry = lax.broadcasted_iota(jnp.int32, (HEAD, 512), 0)
    turn = (entry == jnp.bitwise_or((column >> 5) << 2, jnp.bitwise_and(column, 3))).astype(
        jnp.bfloat16
    )
    high = jnp.dot(leads[:, 0, :], turn, preferred_element_type=jnp.float32)
    low = jnp.dot(leads[:, 1, :], turn, preferred_element_type=jnp.float32)
    place = lax.broadcasted_iota(jnp.int32, (8, 512), 0)
    from_ctx = jnp.bitwise_and(lax.broadcasted_iota(jnp.int32, (8, 512), 1) >> 2, 7)
    slots = jnp.sum(
        jnp.where(place == from_ctx, high * 16 + low, 0.0), axis=0, keepdims=True
    ).astype(jnp.int32)
    pick = (lax.broadcasted_iota(jnp.int32, (512, 512), 0) == slots - 1).astype(jnp.bfloat16)
    for c in range(8):
        takes[c].wait()
        part = jnp.dot(pick, rows[c], preferred_element_type=jnp.float32).astype(jnp.bfloat16)
        out[:, c * HEAD : (c + 1) * HEAD] = part[:, :HEAD]
        out[:, (8 + c) * HEAD : (9 + c) * HEAD] = part[:, HEAD:]


def fill_cache(leads, got):
    return call(
        cache_kernel,
        shape(512, 2048),
        [WHOLE, FAR],
        WHOLE,
        10,
        (2 * 512 * 512 * 2048, 4),
        "fill_cache",
        [pltpu.VMEM((8, 512, 2 * HEAD), jnp.bfloat16), pltpu.SemaphoreType.DMA((8,))],
    )(leads, got)


def spread_kernel(ctx_of, *refs):
    out, leads = refs[-2:]
    side = 0
    for ref in refs[:-2]:
        for i in range(ref.shape[0]):
            ctx = ctx_of[side]
            to = pl.ds(pl.multiple_of(ctx * 2 * HEAD, 2 * HEAD), 2 * HEAD)
            out[:, to] = ref[i, 0:TOK]
            leads[ctx] = ref[i, TOK:, 0:HEAD]
            side += 1


def spread(ctx_of, parts):
    return call(
        spread_kernel,
        [shape(TOK, 2048), shape(8, ROUTE, HEAD)],
        [pl.BlockSpec(memory_space=pltpu.SMEM)] + [WHOLE] * len(parts),
        [WHOLE] * 2,
        6,
        (0, 2),
        "spread",
    )(ctx_of, *parts)


def choose(index, table):
    hit = index[:, None] == jnp.arange(table.shape[0], dtype=jnp.int32)[None, :]
    return jnp.sum(jnp.where(hit, table[None], 0), axis=1, dtype=jnp.int32)


def shards(
    hidden, norm_gain, w_query, w_key, w_value, q_gain, k_gain, lengths, piece_map, owner, slot
):
    y, core = lax.axis_index("y"), lax.axis_index("core")
    group = lax.axis_index(FSDP)
    own = owner[0, 0]
    offsets = jnp.array([0, 1, 3, 2], jnp.int32)

    my_pieces = lax.dynamic_index_in_dim(piece_map, group, 0, keepdims=False)
    my_lengths = lax.dynamic_index_in_dim(lengths, group, 0, keepdims=False)
    ends = jnp.cumsum(my_lengths, dtype=jnp.int32)
    starts = ends - my_lengths
    y_of_pair = ((y + offsets) % 4).astype(jnp.int32)
    core_of = jnp.stack([core, 1 - core]).astype(jnp.int32)
    ctx_of_slot = (y_of_pair[:, None] * 2 + core_of[None, :]).reshape(-1)
    piece_of_slot = choose(ctx_of_slot, my_pieces)
    eight = jnp.arange(8, dtype=jnp.int32)

    def begin_of(places):
        reached = starts[None, :] <= places.reshape(-1, 1)
        return jnp.max(jnp.where(reached, starts[None, :], 0), axis=1).reshape(places.shape)

    low = begin_of(eight * TOK) // TOK
    places = piece_of_slot[:, None] * TOK + jnp.arange(TOK, dtype=jnp.int32)[None, :]
    relative = places - begin_of(places)
    frequency = jnp.exp(jnp.arange(HEAD // 2, dtype=jnp.float32) * (-2.0 * math.log(THETA) / HEAD))
    angles = relative.astype(jnp.float32).reshape(4, 2 * TOK, 1) * frequency
    cos, sin = jnp.cos(angles), jnp.sin(angles)
    cos = jnp.concatenate([cos, cos], axis=-1)
    sin = jnp.concatenate([-sin, sin], axis=-1)

    h = pack(hidden[0, 0], own[None], norm_gain[None])
    above, below = shift(h, "y", -1), shift(h, "y", 1)
    above, below, cos, sin = lax.optimization_barrier((above, below, cos, sin))
    near, half = h, TOK // 2
    far_lo, far_hi = shift(above[:half], "y", -1), shift(below[half:], "y", 1)
    swap = lambda value: shift(value, "core", 1)
    pairs = [
        (near, swap(near)),
        (above, swap(above)),
        (below, swap(below)),
        (far_lo, far_hi, swap(far_lo), swap(far_hi)),
    ]

    token = jnp.arange(TOK, dtype=jnp.int32)
    same = (own[:, None] == own[None, :]) & (token[None, :] < token[:, None])
    rank = jnp.sum(same.astype(jnp.int32), axis=1, dtype=jnp.int32)
    spot = (own % 16) * 32 + (own // 16) * MOST + rank
    hit = spot[None, :] == jnp.arange(512, dtype=jnp.int32)[:, None]
    table = jnp.sum(jnp.where(hit, slot[0, 0][None, :] + 1, 0), axis=1, dtype=jnp.int32)
    table = table.reshape(16, 1, 32)
    table = jnp.concatenate([table // 16, table % 16], axis=1).astype(jnp.bfloat16)
    table = jnp.pad(table, ((0, 0), (0, ROUTE - 2), (0, HEAD - 32)))
    _, table = lax.optimization_barrier((h, table))
    w = spread_weights(w_query, w_key, w_value, table)
    w = lax.all_to_all(w, FSDP, split_axis=0, concat_axis=0, tiled=True)
    leads = w[:, 128:130, :32].reshape(16, 2, 8, MOST).transpose(2, 1, 0, 3).reshape(8, 2, 64)
    leads = jnp.pad(leads, ((0, 0), (0, ROUTE - 2), (0, 2 * HEAD - 64)))

    core = core.astype(jnp.int32)[None]
    k, v, buckets = keys(y_of_pair, piece_of_slot, core, pairs, w, k_gain[None], cos, sin)
    got = lax.all_to_all(buckets, CTX + FSDP, split_axis=0, concat_axis=0, tiled=True)
    maps = piece_of_slot, ctx_of_slot, low, starts
    rest = w, q_gain[None], cos, sin, k, v, leads
    far = [(far_lo, far_hi), (pairs[3][2], pairs[3][3])]
    late = attend(4, [(x,) for x in pairs[2]] + far, *maps, *rest)
    late = late.reshape(2, 2, TOK + ROUTE, 2 * HEAD)
    from_above = shift(late, "y", -1)
    mixed = attend(0, [(x,) for x in pairs[0] + pairs[1]], *maps, *rest)
    mixed = mixed.reshape(2, 2, TOK + ROUTE, 2 * HEAD)
    from_below = shift(mixed[1], "y", 1)
    from_far = shift(from_above[1], "y", -1)
    mine = [mixed[0], from_above[0], from_below, from_far]
    other = [swap(m[1]) for m in mine]
    parts = [p for m, o in zip(mine, other) for p in (m[0][None], o[None])]
    attended, leads = spread(ctx_of_slot, parts)
    cache = fill_cache(leads, got.reshape(8, 512, 2 * HEAD))
    return attended[None, None], cache


def solution(mesh):
    split = Mesh(mesh.devices.reshape(4, 2, 4, 4), (*CTX, *FSDP))
    placed = (
        P(CTX, FSDP, None, None),
        P(),
        P(FSDP, CTX),
        P(FSDP, CTX),
        P(FSDP, CTX),
        P(),
        P(),
        P(),
        P(),
        P(CTX, FSDP, None),
        P(CTX, FSDP, None),
    )
    return jax.shard_map(
        shards,
        mesh=split,
        in_specs=placed,
        out_specs=(P(CTX, FSDP, None, None), P((*CTX, *FSDP), None)),
        check_vma=False,
    )
```

```python
import math

import jax
import jax.numpy as jnp
from jax import lax
from jax.experimental import pallas as pl
from jax.experimental.pallas import tpu as pltpu
from jax.sharding import Mesh, PartitionSpec as P

HEAD = 128
TOK = 256
EPSILON = 1e-06
THETA = 1000000.0
NEG_BIG = -1e30
MOST = 4
MIB = 1 << 20
ROUTE = 8
CTX = ("y", "core")
FSDP = ("x", "z")


def shift(value, axis, by):
    size = lax.axis_size(axis)
    return lax.ppermute(value, axis, [(i, (i + by) % size) for i in range(size)])


def norm_rope(raw, gain, cos, sin):
    factor = lax.rsqrt(jnp.mean(raw * raw, axis=-1, keepdims=True) + EPSILON)
    normal = raw * factor * gain
    return (normal * cos + pltpu.roll(normal, HEAD // 2, 1) * sin).astype(jnp.bfloat16)


def call(kernel, out_shape, specs, outs, mib, cost, name, scratch=(), grid=(), maps=()):
    flops, moved = cost
    return pl.pallas_call(
        kernel,
        grid_spec=pltpu.PrefetchScalarGridSpec(
            num_scalar_prefetch=len(maps),
            grid=grid,
            in_specs=specs,
            out_specs=outs,
            scratch_shapes=scratch,
        ),
        out_shape=out_shape,
        compiler_params=pltpu.CompilerParams(vmem_limit_bytes=mib * MIB),
        cost_estimate=pl.CostEstimate(flops=flops, bytes_accessed=moved * MIB, transcendentals=0),
        name=name,
    )


def shape(*dims, dtype=jnp.bfloat16):
    return jax.ShapeDtypeStruct(dims, dtype)


WHOLE = pl.BlockSpec(memory_space=pltpu.VMEM)
FAR = pl.BlockSpec(memory_space=pltpu.HBM)


def pack_kernel(hidden, own_hbm, gain_hbm, out, x, own, gain, sems):
    first = pltpu.make_async_copy(own_hbm, own, sems.at[0])
    move = pltpu.make_async_copy(hidden, x, sems.at[1])
    last = pltpu.make_async_copy(gain_hbm, gain, sems.at[2])
    first.start()
    move.start()
    last.start()
    first.wait()
    row = own[...].astype(jnp.float32)
    column = jnp.transpose(jnp.broadcast_to(row, (ROUTE, TOK)))[:, 0:1]
    token = lax.broadcasted_iota(jnp.int32, (TOK, TOK), 0)
    other = lax.broadcasted_iota(jnp.int32, (TOK, TOK), 1)
    same = (column == row) & (token < other)
    rank = jnp.sum(same.astype(jnp.float32), axis=0, keepdims=True)
    out[TOK:, :] = jnp.zeros((ROUTE, out.shape[1]), out.dtype)
    which = lax.broadcasted_iota(jnp.int32, (ROUTE, TOK), 0)
    lead = jnp.where(which == 0, row, jnp.where(which == 1, rank, 0.0))
    out[TOK:, 0:TOK] = lead.astype(out.dtype)
    move.wait()
    last.wait()
    for i in range(0, TOK, 128):
        part = x[i : i + 128, :].astype(jnp.float32)
        factor = lax.rsqrt(jnp.mean(part * part, axis=-1, keepdims=True) + EPSILON)
        out[i : i + 128, :] = (part * factor * gain[...]).astype(out.dtype)


def pack(hidden, own, gain):
    return call(
        pack_kernel,
        shape(TOK + ROUTE, 2048),
        [FAR, FAR, FAR],
        WHOLE,
        58,
        (0, 2),
        "pack",
        [
            pltpu.VMEM((TOK, 2048), jnp.bfloat16),
            pltpu.VMEM((1, TOK), jnp.int32),
            pltpu.VMEM((1, 2048), jnp.float32),
            pltpu.SemaphoreType.DMA((3,)),
        ],
    )(hidden, own, gain)


def spread_weights_kernel(a, b, c, routes, out, part, sems):
    moves = [
        pltpu.make_async_copy(a, part.at[:, pl.ds(0, 2 * HEAD)], sems.at[0]),
        pltpu.make_async_copy(b, part.at[:, pl.ds(2 * HEAD, HEAD)], sems.at[1]),
        pltpu.make_async_copy(c, part.at[:, pl.ds(3 * HEAD, HEAD)], sems.at[2]),
    ]
    for move in moves:
        move.start()
    for i in range(16):
        out[i, 128:, 0:HEAD] = routes[i]
        out[i, 128:, HEAD:] = jnp.zeros((ROUTE, 3 * HEAD), out.dtype)
    for move in moves:
        move.wait()
    for i in range(16):
        out[i, 0:128, :] = part[...]


def spread_weights(a, b, c, routes):
    return call(
        spread_weights_kernel,
        shape(16, 128 + ROUTE, 4 * HEAD),
        [FAR, FAR, FAR, WHOLE],
        WHOLE,
        6,
        (0, 3),
        "spread_weights",
        [pltpu.VMEM((128, 4 * HEAD), jnp.bfloat16), pltpu.SemaphoreType.DMA((3,))],
    )(a, b, c, routes)


def data_rows(ref):
    return ref.shape[0] - ref.shape[0] % 16


def take_weights(got, part, out):
    for i in range(16):
        out[i * 128 : (i + 1) * 128, :] = got[i, 0:128, part]


def keys(y_of_pair, piece_of, core, pairs, w, gain, cos, sin):
    count = sum(len(p) for p in pairs)

    def kernel(ys, piece, core_ref, *refs):
        w_ref, gain_ref, cos_ref, sin_ref, k_hbm, v_hbm, b_hbm = refs[count : count + 7]
        w_kv, kv, k_out, v_out, b_out, sems, xs, takes = refs[count + 7 :]
        step = pl.program_id(0)

        def send(i):
            at = pl.multiple_of(ys[i] * 8, 8)
            return pltpu.make_async_copy(b_out.at[i], b_hbm.at[:, pl.ds(at, 8), :], sems.at[i])

        def fetch(i):
            first = sum(len(p) for p in pairs[:i])
            moves = []
            row, side = 0, 0
            for n in range(first, first + len(pairs[i])):
                height = refs[n].shape[0]
                to = xs.at[2 * i + side, pl.ds(row, height)]
                moves.append(pltpu.make_async_copy(refs[n], to, takes.at[n]))
                row += height
                if row == TOK + ROUTE:
                    row, side = 0, side + 1
            return moves

        @pl.when(step == 0)
        def _():
            for i in range(len(pairs)):
                for move in fetch(i):
                    move.start()
            take_weights(w_ref, slice(2 * HEAD, 4 * HEAD), w_kv)

        def arrive(i):
            for move in fetch(i):
                move.wait()

        for i in range(len(pairs)):
            pl.when(step == i)(lambda i=i: arrive(i))

        def go():
            codes = []
            for side in range(2):
                x = 2 * step + side
                raw = jnp.dot(xs[x, 0:TOK, :], w_kv[...], preferred_element_type=jnp.float32)
                put = slice(side * TOK, (side + 1) * TOK)
                kv[put, :HEAD] = norm_rope(
                    raw[:, :HEAD], gain_ref[...], cos_ref[0, put, :], sin_ref[0, put, :]
                )
                kv[put, HEAD:] = raw[:, HEAD:].astype(jnp.bfloat16)
                lead = xs[x, TOK:, 0:TOK].astype(jnp.float32)
                mine = core_ref[0] + side - 2 * core_ref[0] * side
                codes.append((lead[0:1] * 8 + lead[1:2]).astype(jnp.int32) + mine * MOST)
            place = lax.broadcasted_iota(jnp.int32, (8 * 128, 2 * TOK), 0)
            pick = (place == jnp.concatenate(codes, axis=1)).astype(jnp.bfloat16)
            got = jnp.dot(pick, kv[...], preferred_element_type=jnp.float32)
            b_out[step] = got.reshape(128, 8, 2 * HEAD).astype(jnp.bfloat16)
            send(step).start()
            for side in range(2):
                to = pl.ds(pl.multiple_of(piece[2 * step + side] * TOK, TOK), TOK)
                k_out[to, :] = kv[side * TOK : (side + 1) * TOK, :HEAD]
                v_out[to, :] = kv[side * TOK : (side + 1) * TOK, HEAD:]

        go()

        @pl.when(step == 3)
        def _():
            last = [
                pltpu.make_async_copy(k_out, k_hbm, sems.at[4]),
                pltpu.make_async_copy(v_out, v_hbm, sems.at[5]),
            ]
            for move in last:
                move.start()
            for i in range(4):
                send(i).wait()
            for move in last:
                move.wait()

    maps = y_of_pair, piece_of, core
    table = pl.BlockSpec((1, 2 * TOK, HEAD), lambda i, *_: (i, 0, 0))
    return call(
        kernel,
        [
            pltpu.HBM((8 * TOK, HEAD), jnp.bfloat16),
            pltpu.HBM((8 * TOK, HEAD), jnp.bfloat16),
            pltpu.HBM((128, 32, 2 * HEAD), jnp.bfloat16),
        ],
        [FAR] * count + [WHOLE] * 2 + [table] * 2,
        [FAR] * 3,
        26,
        (2 * 2048 * 2048 * 256, 12),
        "keys",
        [
            pltpu.VMEM((2048, 2 * HEAD), jnp.bfloat16),
            pltpu.VMEM((2 * TOK, 2 * HEAD), jnp.bfloat16),
            pltpu.VMEM((8 * TOK, HEAD), jnp.bfloat16),
            pltpu.VMEM((8 * TOK, HEAD), jnp.bfloat16),
            pltpu.VMEM((4, 128, 8, 2 * HEAD), jnp.bfloat16),
            pltpu.SemaphoreType.DMA((6,)),
            pltpu.VMEM((8, TOK + ROUTE, 2048), jnp.bfloat16),
            pltpu.SemaphoreType.DMA((count,)),
        ],
        (4,),
        maps,
    )(*maps, *(x for p in pairs for x in p), w, gain, cos, sin)


def attend(first, pieces, piece_of, ctx_of, low, starts, w, gain, cos, sin, k, v, leads):
    count = sum(len(p) for p in pieces)

    def kernel(piece, ctx, lows, begins, *refs):
        w_ref, gain_ref, cos_ref, sin_ref, k_hbm, v_hbm, lead, out = refs[count : count + 8]
        w_q, both, keys_ref, values, sems = refs[count + 8 :]
        step = pl.program_id(0)
        moves = [
            pltpu.make_async_copy(k_hbm, keys_ref, sems.at[0]),
            pltpu.make_async_copy(v_hbm, values, sems.at[1]),
        ]

        @pl.when(step == 0)
        def _():
            for move in moves:
                move.start()
            take_weights(w_ref, slice(0, 2 * HEAD), w_q)

        def query(part):
            at = 0
            for ref in part:
                rows = data_rows(ref)
                raw = jnp.dot(ref[0:rows, :], w_q[...], preferred_element_type=jnp.float32)
                put = slice(at, at + rows)
                for h in range(2):
                    both[h * TOK + at : h * TOK + at + rows, :] = norm_rope(
                        raw[:, h * HEAD : (h + 1) * HEAD],
                        gain_ref[...],
                        cos_ref[0, put, :],
                        sin_ref[0, put, :],
                    )
                at += rows

        at = 0
        for i, p in enumerate(pieces):
            pl.when(step == i)(lambda part=refs[at : at + len(p)]: query(part))
            at += len(p)

        @pl.when(step == 0)
        def _():
            for move in moves:
                move.wait()

        p = piece[first + step]
        lo = lows[p]
        out[0, TOK:, :] = lead[0]
        place = p * TOK + lax.broadcasted_iota(jnp.int32, (TOK, 1), 0)
        begin = jnp.zeros_like(place)
        for n in range(1, 4):
            begin = jnp.where(begins[n] <= place, begins[n], begin)

        def blocks(span):
            at = pl.multiple_of(lo * TOK, TOK)
            spot = at + lax.broadcasted_iota(jnp.int32, (1, span), 1)
            seen = (spot <= place) & (spot >= begin)
            for h in range(2):
                s = lax.dot_general(
                    both[h * TOK : (h + 1) * TOK],
                    keys_ref[pl.ds(at, span), :],
                    (((1,), (1,)), ((), ())),
                    preferred_element_type=jnp.float32,
                )
                s = jnp.where(seen, s, NEG_BIG)
                top = jnp.max(s, axis=1, keepdims=True)
                e = jnp.exp((s - top) * (1.0 / math.sqrt(HEAD)))
                total = jnp.sum(e, axis=1, keepdims=True)
                mixed = jnp.dot(
                    e.astype(jnp.bfloat16),
                    values[pl.ds(at, span), :],
                    preferred_element_type=jnp.float32,
                )
                out[0, 0:TOK, h * HEAD : (h + 1) * HEAD] = (mixed / total).astype(jnp.bfloat16)

        for n in range(1, 6):
            pl.when(p + 1 - lo == n)(lambda n=n: blocks(n * TOK))

    maps = piece_of, ctx_of, low, starts
    n = len(pieces)
    table = pl.BlockSpec((1, TOK, HEAD), lambda i, *_: (first // 2 + i // 2, i % 2, 0))
    return call(
        kernel,
        shape(n, TOK + ROUTE, 2 * HEAD),
        [WHOLE] * (count + 2)
        + [table] * 2
        + [FAR] * 2
        + [pl.BlockSpec((1, ROUTE, 2 * HEAD), lambda i, p, c, *_: (c[first + i], 0, 0))],
        pl.BlockSpec((1, TOK + ROUTE, 2 * HEAD), lambda i, *_: (i, 0, 0)),
        16,
        (n * 2048 * 2048 * 128, 4),
        "attend",
        [
            pltpu.VMEM((2048, 2 * HEAD), jnp.bfloat16),
            pltpu.VMEM((2 * TOK, HEAD), jnp.bfloat16),
            pltpu.VMEM((8 * TOK, HEAD), jnp.bfloat16),
            pltpu.VMEM((8 * TOK, HEAD), jnp.bfloat16),
            pltpu.SemaphoreType.DMA((2,)),
        ],
        (n,),
        maps,
    )(
        *maps,
        *(x for p in pieces for x in p),
        w,
        gain,
        cos,
        sin,
        k,
        v,
        leads,
    )


def cache_kernel(leads, got, out, rows, in_sems):
    takes = [pltpu.make_async_copy(got.at[c], rows.at[c], in_sems.at[c]) for c in range(8)]
    for take in takes:
        take.start()
    column = lax.broadcasted_iota(jnp.int32, (HEAD, 512), 1)
    entry = lax.broadcasted_iota(jnp.int32, (HEAD, 512), 0)
    turn = (entry == jnp.bitwise_or((column >> 5) << 2, jnp.bitwise_and(column, 3))).astype(
        jnp.bfloat16
    )
    high = jnp.dot(leads[:, 0, :], turn, preferred_element_type=jnp.float32)
    low = jnp.dot(leads[:, 1, :], turn, preferred_element_type=jnp.float32)
    place = lax.broadcasted_iota(jnp.int32, (8, 512), 0)
    from_ctx = jnp.bitwise_and(lax.broadcasted_iota(jnp.int32, (8, 512), 1) >> 2, 7)
    slots = jnp.sum(
        jnp.where(place == from_ctx, high * 16 + low, 0.0), axis=0, keepdims=True
    ).astype(jnp.int32)
    pick = (lax.broadcasted_iota(jnp.int32, (512, 512), 0) == slots - 1).astype(jnp.bfloat16)
    for c in range(8):
        takes[c].wait()
        part = jnp.dot(pick, rows[c], preferred_element_type=jnp.float32).astype(jnp.bfloat16)
        out[:, c * HEAD : (c + 1) * HEAD] = part[:, :HEAD]
        out[:, (8 + c) * HEAD : (9 + c) * HEAD] = part[:, HEAD:]


def fill_cache(leads, got):
    return call(
        cache_kernel,
        shape(512, 2048),
        [WHOLE, FAR],
        WHOLE,
        10,
        (2 * 512 * 512 * 2048, 4),
        "fill_cache",
        [pltpu.VMEM((8, 512, 2 * HEAD), jnp.bfloat16), pltpu.SemaphoreType.DMA((8,))],
    )(leads, got)


def spread_kernel(ctx_of, *refs):
    out, leads = refs[-2:]
    side = 0
    for ref in refs[:-2]:
        for i in range(ref.shape[0]):
            ctx = ctx_of[side]
            to = pl.ds(pl.multiple_of(ctx * 2 * HEAD, 2 * HEAD), 2 * HEAD)
            out[:, to] = ref[i, 0:TOK]
            leads[ctx] = ref[i, TOK:, 0:HEAD]
            side += 1


def spread(ctx_of, parts):
    return call(
        spread_kernel,
        [shape(TOK, 2048), shape(8, ROUTE, HEAD)],
        [pl.BlockSpec(memory_space=pltpu.SMEM)] + [WHOLE] * len(parts),
        [WHOLE] * 2,
        6,
        (0, 2),
        "spread",
    )(ctx_of, *parts)


def choose(index, table):
    hit = index[:, None] == jnp.arange(table.shape[0], dtype=jnp.int32)[None, :]
    return jnp.sum(jnp.where(hit, table[None], 0), axis=1, dtype=jnp.int32)


def shards(
    hidden, norm_gain, w_query, w_key, w_value, q_gain, k_gain, lengths, piece_map, owner, slot
):
    y, core = lax.axis_index("y"), lax.axis_index("core")
    group = lax.axis_index(FSDP)
    own = owner[0, 0]
    offsets = jnp.array([0, 1, 3, 2], jnp.int32)

    my_pieces = lax.dynamic_index_in_dim(piece_map, group, 0, keepdims=False)
    my_lengths = lax.dynamic_index_in_dim(lengths, group, 0, keepdims=False)
    ends = jnp.cumsum(my_lengths, dtype=jnp.int32)
    starts = ends - my_lengths
    y_of_pair = ((y + offsets) % 4).astype(jnp.int32)
    core_of = jnp.stack([core, 1 - core]).astype(jnp.int32)
    ctx_of_slot = (y_of_pair[:, None] * 2 + core_of[None, :]).reshape(-1)
    piece_of_slot = choose(ctx_of_slot, my_pieces)
    eight = jnp.arange(8, dtype=jnp.int32)

    def begin_of(places):
        reached = starts[None, :] <= places.reshape(-1, 1)
        return jnp.max(jnp.where(reached, starts[None, :], 0), axis=1).reshape(places.shape)

    low = begin_of(eight * TOK) // TOK
    places = piece_of_slot[:, None] * TOK + jnp.arange(TOK, dtype=jnp.int32)[None, :]
    relative = places - begin_of(places)
    frequency = jnp.exp(jnp.arange(HEAD // 2, dtype=jnp.float32) * (-2.0 * math.log(THETA) / HEAD))
    angles = relative.astype(jnp.float32).reshape(4, 2 * TOK, 1) * frequency
    cos, sin = jnp.cos(angles), jnp.sin(angles)
    cos = jnp.concatenate([cos, cos], axis=-1)
    sin = jnp.concatenate([-sin, sin], axis=-1)

    h = pack(hidden[0, 0], own[None], norm_gain[None])
    above, below = shift(h, "y", -1), shift(h, "y", 1)
    above, below, cos, sin = lax.optimization_barrier((above, below, cos, sin))
    near, half = h, TOK // 2
    far_lo, far_hi = shift(above[:half], "y", -1), shift(below[half:], "y", 1)
    swap = lambda value: shift(value, "core", 1)
    pairs = [
        (near, swap(near)),
        (above, swap(above)),
        (below, swap(below)),
        (far_lo, far_hi, swap(far_lo), swap(far_hi)),
    ]

    token = jnp.arange(TOK, dtype=jnp.int32)
    same = (own[:, None] == own[None, :]) & (token[None, :] < token[:, None])
    rank = jnp.sum(same.astype(jnp.int32), axis=1, dtype=jnp.int32)
    spot = (own % 16) * 32 + (own // 16) * MOST + rank
    hit = spot[None, :] == jnp.arange(512, dtype=jnp.int32)[:, None]
    table = jnp.sum(jnp.where(hit, slot[0, 0][None, :] + 1, 0), axis=1, dtype=jnp.int32)
    table = table.reshape(16, 1, 32)
    table = jnp.concatenate([table // 16, table % 16], axis=1).astype(jnp.bfloat16)
    table = jnp.pad(table, ((0, 0), (0, ROUTE - 2), (0, HEAD - 32)))
    _, table = lax.optimization_barrier((h, table))
    w = spread_weights(w_query, w_key, w_value, table)
    w = lax.all_to_all(w, FSDP, split_axis=0, concat_axis=0, tiled=True)
    leads = w[:, 128:130, :32].reshape(16, 2, 8, MOST).transpose(2, 1, 0, 3).reshape(8, 2, 64)
    leads = jnp.pad(leads, ((0, 0), (0, ROUTE - 2), (0, 2 * HEAD - 64)))

    core = core.astype(jnp.int32)[None]
    k, v, buckets = keys(y_of_pair, piece_of_slot, core, pairs, w, k_gain[None], cos, sin)
    got = lax.all_to_all(buckets, CTX + FSDP, split_axis=0, concat_axis=0, tiled=True)
    maps = piece_of_slot, ctx_of_slot, low, starts
    rest = w, q_gain[None], cos, sin, k, v, leads
    far = [(far_lo, far_hi), (pairs[3][2], pairs[3][3])]
    late = attend(4, [(x,) for x in pairs[2]] + far, *maps, *rest)
    late = late.reshape(2, 2, TOK + ROUTE, 2 * HEAD)
    from_above = shift(late, "y", -1)
    mixed = attend(0, [(x,) for x in pairs[0] + pairs[1]], *maps, *rest)
    mixed = mixed.reshape(2, 2, TOK + ROUTE, 2 * HEAD)
    from_below = shift(mixed[1], "y", 1)
    from_far = shift(from_above[1], "y", -1)
    mine = [mixed[0], from_above[0], from_below, from_far]
    other = [swap(m[1]) for m in mine]
    parts = [p for m, o in zip(mine, other) for p in (m[0][None], o[None])]
    attended, leads = spread(ctx_of_slot, parts)
    cache = fill_cache(leads, got.reshape(8, 512, 2 * HEAD))
    return attended[None, None], cache


def solution(mesh):
    split = Mesh(mesh.devices.reshape(4, 2, 4, 4), (*CTX, *FSDP))
    placed = (
        P(CTX, FSDP, None, None),
        P(),
        P(FSDP, CTX),
        P(FSDP, CTX),
        P(FSDP, CTX),
        P(),
        P(),
        P(),
        P(),
        P(CTX, FSDP, None),
        P(CTX, FSDP, None),
    )
    return jax.shard_map(
        shards,
        mesh=split,
        in_specs=placed,
        out_specs=(P(CTX, FSDP, None, None), P((*CTX, *FSDP), None)),
        check_vma=False,
    )
```
